32 devices in a mesh: item: 4 (over y, x), user: 4 (over z), edge: 2 (over core).
Axes of the slice: x: 2, y: 2, z: 4, core: 2. Of those that a mesh axis runs over, the one named last changes fastest.
Arguments:
- item_emb: bfloat16 [16384, 256], P('item'), may hold values from -6 to 6
- user_emb: bfloat16 [24576, 256], P('user'), may hold values from -6 to 6
- block_item: int32 [4, 4, 2, 96], P('item', 'user', 'edge'), may hold values from 0 to 31
- block_user: int32 [4, 4, 2, 96], P('item', 'user', 'edge'), may hold values from 0 to 47
- block_rows: int32 [4, 4, 2, 96, 128], P('item', 'user', 'edge'), may hold values from 0 to 127
- block_count: int32 [4, 4, 2], P('item', 'user', 'edge'), may hold values from 1 to 96, as said below
- user_weight: bfloat16 [256, 256], replicated, may hold values from -3.5 to 3.5
- up_weight: bfloat16 [256, 1024], replicated, may hold values from -0.375 to 0.375
- down_weight: bfloat16 [1024, 256], replicated, may hold values from -0.1875 to 0.1875
Outputs:
- new_items: bfloat16 [16384, 256], P(('item', 'user', 'edge'))
The draws below stay inside these ranges and needn't reach their ends.
Inputs may be any that keep to these rules, and one draw needn't show every extreme that they name: `block_count`: some list has exactly 96 live slots in every draw; entries of slots that are not live are ignored.
All inputs are finite; a program needn't handle non-finite values.
Results may differ from the reference program's by a relative error of at most 0.0045.
Values may be sent and summed in bfloat16 or wider, within the bound.
No kernel may reach another device: no remote copies, remote signals or barrier semaphores. Data moves between devices by JAX's collectives and lax.ppermute only.
A program may use at most 64 MiB of HBM per device.

```python
import jax
import jax.numpy as jnp
from jax import lax

E = 256
HID = 1024
TILE = 128
IT_SH = 32
US_SH = 48
MAXB = 96
GI = 4
GU = 4
GE = 2
ITEMS = 16384
USERS = 24576
USER_DEGREE = 10


def draw_block_count(key, part):
    first, second = jax.random.split(jax.random.fold_in(key, 17))
    lowest = max(1, MAXB // 4)
    counts = jax.random.randint(first, (GI * GU * GE,), lowest, MAXB + 1, dtype=jnp.int32)
    chosen = jax.random.randint(second, (), 0, GI * GU * GE, dtype=jnp.int32)
    counts = jnp.where(jnp.arange(GI * GU * GE, dtype=jnp.int32) == chosen, MAXB, counts)
    return counts.reshape(GI, GU, GE)


def plant(values, key, low, high):
    place = [jax.random.randint(jax.random.fold_in(key, axis), (), 0, length) for axis, length in enumerate(values.shape)]
    widest = values.shape.index(max(values.shape))
    neighbour = place[:widest] + [(place[widest] + 1) % values.shape[widest]] + place[widest + 1:]
    return values.at[tuple(place)].set(low).at[tuple(neighbour)].set(high)


def block_levels(key, shape, pieces, low, top_value):
    def one(axis_at, shards_of):
        steps = jax.random.uniform(jax.random.fold_in(jax.random.fold_in(key, 6), axis_at), (shards_of,), jnp.float32, low / len(pieces), top_value / len(pieces))
        return jnp.repeat(jnp.exp(steps), shape[axis_at] // shards_of).reshape((-1,) + (1,) * (len(shape) - axis_at - 1))

    loudness = one(*pieces[0])
    for cut in pieces[1:]:
        loudness = loudness * one(*cut)
    return loudness


def centred(own_key, extent, deviation, most, pieces=(), kind=jnp.bfloat16):
    loudness = block_levels(own_key, extent, pieces, -0.22, 0.18) if pieces else 1.0
    entries = jax.random.normal(own_key, extent, jnp.float32) * deviation * loudness
    return jnp.minimum(jnp.maximum(entries, -most), most).astype(kind)


def setup_inputs(seed: int = 0) -> dict:
    keys = jax.random.split(jax.random.key(seed), 10)
    return {
        "item_emb": centred(keys[0], (ITEMS, E), 1.0, 6.0, ((0, 4),)),
        "user_emb": centred(keys[1], (USERS, E), 1.0, 6.0, ((0, 4),)),
        "block_item": plant(jax.random.randint(keys[2], (GI, GU, GE, MAXB), 0, IT_SH), jax.random.fold_in(keys[2], 1), 0, IT_SH - 1).astype(jnp.int32),
        "block_user": plant(jax.random.randint(keys[3], (GI, GU, GE, MAXB), 0, US_SH), jax.random.fold_in(keys[3], 1), 0, US_SH - 1).astype(jnp.int32),
        "block_rows": plant(jax.random.randint(keys[4], (GI, GU, GE, MAXB, TILE), 0, TILE), jax.random.fold_in(keys[4], 1), 0, TILE - 1).astype(jnp.int32),
        "block_count": draw_block_count(jax.random.fold_in(keys[9], 71), 0),
        "user_weight": centred(keys[6], (E, E), (3.0 * USER_DEGREE ** 0.5 * E ** -0.5), 3.5),
        "up_weight": centred(keys[7], (E, HID), E ** -0.5, 0.375),
        "down_weight": centred(keys[8], (HID, E), HID ** -0.5, 0.1875),
    }


def reference(item_emb, user_emb, block_item, block_user, block_rows, block_count, user_weight, up_weight, down_weight):
    item_span = IT_SH * TILE
    user_span = US_SH * TILE
    lists = GI * GU * GE
    slot_items = block_item.reshape(lists, MAXB)
    slot_users = block_user.reshape(lists, MAXB)
    slot_links = block_rows.reshape(lists, MAXB, TILE)
    counts = block_count.reshape(lists)
    numbers = jnp.arange(lists, dtype=jnp.int32)
    inside = jnp.arange(TILE, dtype=jnp.int32)
    positions = jnp.arange(MAXB, dtype=jnp.int32)

    def edges_of(which, items_at, users_at, links, live_count):
        owner_item = which // (GU * GE)
        owner_user = (which // GE) % GU
        source_rows = owner_item * item_span + items_at[:, None] * TILE + inside[None, :]
        target_rows = owner_user * user_span + users_at[:, None] * TILE + links
        alive = jnp.broadcast_to((positions < live_count)[:, None], (MAXB, TILE)).astype(jnp.float32)
        return source_rows.reshape(-1).astype(jnp.int32), target_rows.reshape(-1).astype(jnp.int32), alive.reshape(-1)

    def first_hop(carry, packed):
        summed, degree = carry
        source_rows, target_rows, alive = edges_of(*packed)
        values = item_emb[source_rows].astype(jnp.float32) * alive[:, None]
        return (summed.at[target_rows].add(values), degree.at[target_rows].add(alive)), None

    start = (jnp.zeros((USERS, E), jnp.float32), jnp.zeros((USERS,), jnp.float32))
    (user_sum, user_degree), _ = lax.scan(first_hop, start, (numbers, slot_items, slot_users, slot_links, counts))
    user_mean = (user_sum / jnp.maximum(user_degree, 1.0)[:, None]).astype(jnp.bfloat16)
    user_new = (user_emb.astype(jnp.float32) + jax.nn.silu(jnp.dot(user_mean, user_weight, preferred_element_type=jnp.float32))).astype(jnp.bfloat16)

    def second_hop(carry, packed):
        summed, degree = carry
        source_rows, target_rows, alive = edges_of(*packed)
        values = user_new[target_rows].astype(jnp.float32) * alive[:, None]
        return (summed.at[source_rows].add(values), degree.at[source_rows].add(alive)), None

    start = (jnp.zeros((ITEMS, E), jnp.float32), jnp.zeros((ITEMS,), jnp.float32))
    (item_sum, item_degree), _ = lax.scan(second_hop, start, (numbers, slot_items, slot_users, slot_links, counts))
    merged = item_emb.astype(jnp.float32) + item_sum / jnp.maximum(item_degree, 1.0)[:, None]
    hidden = jax.nn.silu(jnp.dot(merged.astype(jnp.bfloat16), up_weight, preferred_element_type=jnp.float32)).astype(jnp.bfloat16)
    return (merged + jnp.dot(hidden, down_weight, preferred_element_type=jnp.float32)).astype(jnp.bfloat16)
```

```python
import functools

import jax
import jax.numpy as jnp
from jax import lax
from jax.experimental import pallas as pl
from jax.experimental.pallas import tpu as pltpu
from jax.sharding import PartitionSpec as P

TILE = 128
GROUP = 8
F32 = jnp.float32
BF16 = jnp.bfloat16
ANY = pl.BlockSpec(memory_space=pl.ANY)
VMEM = pl.BlockSpec(memory_space=pltpu.VMEM)
SMEM = pl.BlockSpec(memory_space=pltpu.SMEM)


def silu(v):
    return v / (1.0 + jnp.exp(-v))


def choose_slots(lists, slots, pick, slot_of, source_of, target_of):
    found = jnp.int32(0)
    for number, (items, users, count) in enumerate(lists):
        live = count[0]

        def step(b, found, number=number, items=items, users=users, live=live):
            source, target, mine = pick(items[b], users[b])
            slot_of[found] = number * slots + b
            source_of[found] = source
            target_of[found] = target
            return found + jnp.where(jnp.logical_and(mine, b < live), 1, 0)

        found = lax.fori_loop(0, slots, step, found, unroll=4)
    for extra in range(GROUP):
        slot_of[found + extra] = len(lists) * slots
        source_of[found + extra] = 0
        target_of[found + extra] = 0
    return (found + GROUP - 1) // GROUP


def load_links(links, held, sem):
    slots = links[0].shape[0]
    copies = []
    for number, ref in enumerate(links):
        copies.append(
            pltpu.make_async_copy(ref, held.at[pl.ds(number * slots, slots)], sem.at[number])
        )
    for copy in copies:
        copy.start()
    tail = len(links) * slots
    held[tail:, :] = jnp.full((held.shape[0] - tail, TILE), -1, jnp.int32)
    return copies


def hop_one_kernel(n_item, n_edge, half_tiles, *refs):
    lists = [refs[3 * e : 3 * e + 3] for e in range(n_edge)]
    refs = refs[3 * n_edge :]
    links, refs = refs[:n_edge], refs[n_edge:]
    items, refs = refs[0], refs[1:]
    pieces, refs = refs[: 2 * n_item], refs[2 * n_item :]
    degree, total, held, rows, slot_of, source_of, target_of, sem = refs
    slots = links[0].shape[0]
    me, core = lax.axis_index("item"), lax.axis_index("edge")
    copies = load_links(links, held, sem)
    copies.append(pltpu.make_async_copy(items, rows, sem.at[n_edge]))
    copies[-1].start()

    def pick(item, user):
        target = user - core * half_tiles
        return item, target, jnp.logical_and(target >= 0, target < half_tiles)

    groups = choose_slots(lists, slots, pick, slot_of, source_of, target_of)
    total[...] = jnp.zeros_like(total)
    degree[...] = jnp.zeros_like(degree)
    for copy in copies:
        copy.wait()
    inside = lax.broadcasted_iota(jnp.int32, (TILE, TILE), 0)
    ones = jnp.ones((8, TILE), BF16)

    def step(g, carry):
        for i in range(GROUP):
            at = g * GROUP + i
            link = held[pl.ds(slot_of[at], 1), :]
            onehot = jnp.where(inside == link, 1.0, 0.0).astype(BF16)
            source = pl.multiple_of(source_of[at] * TILE, TILE)
            target = pl.multiple_of(target_of[at] * TILE, TILE)
            part = jnp.dot(onehot, rows[pl.ds(source, TILE), :], preferred_element_type=F32)
            total[pl.ds(target, TILE), :] += part
            hits = lax.dot_general(
                ones, onehot, (((1,), (1,)), ((), ())), preferred_element_type=F32
            )
            low = pl.multiple_of(target_of[at] * 8, 8)
            degree[pl.ds(low, 8), :] += hits
        return carry

    lax.fori_loop(0, groups, step, 0)
    span = total.shape[0] // n_item
    for k in range(n_item):
        owner = jnp.bitwise_xor(me, k)
        for h in range(2):
            first = pl.multiple_of(owner * span + h * (span // 2), 16)
            out = pieces[2 * k + h]
            out[...] = total[pl.ds(first, span // 2), :].astype(out.dtype)


def hop_one(lists, links, items, n_item, n_edge, user_tiles):
    half_tiles = user_tiles // n_edge
    slots, channels = links[0].shape[0], items.shape[1]
    piece = half_tiles * TILE // n_item // 2
    shapes = [
        jax.ShapeDtypeStruct((piece, channels), F32 if k == 0 else BF16)
        for k in range(n_item)
        for _ in range(2)
    ]
    shapes.append(jax.ShapeDtypeStruct((half_tiles * 8, TILE), F32))
    room = n_edge * slots + GROUP
    return pl.pallas_call(
        functools.partial(hop_one_kernel, n_item, n_edge, half_tiles),
        out_shape=shapes,
        in_specs=[SMEM] * (3 * n_edge) + [ANY] * (n_edge + 1),
        out_specs=[VMEM] * len(shapes),
        scratch_shapes=[
            pltpu.VMEM((half_tiles * TILE, channels), F32),
            pltpu.VMEM((n_edge * slots + 8, TILE), jnp.int32),
            pltpu.VMEM(items.shape, BF16),
            pltpu.SMEM((room,), jnp.int32),
            pltpu.SMEM((room,), jnp.int32),
            pltpu.SMEM((room,), jnp.int32),
            pltpu.SemaphoreType.DMA((n_edge + 1,)),
        ],
        name="hop_one",
    )(*[part for entry in lists for part in entry], *links, items)


def refresh_body(counts, n_degree, half_tiles, *refs):
    low = refs[: counts[0]]
    refs = refs[counts[0] :]
    high = refs[: counts[1]]
    refs = refs[counts[1] :]
    degrees, refs = refs[:n_degree], refs[n_degree:]
    weight, emb, out_low, out_high, own, inverse, sem = refs
    me, core = lax.axis_index("item"), lax.axis_index("edge")
    piece = out_low.shape[0]
    first = core * half_tiles * TILE + me * 2 * piece
    copy = pltpu.make_async_copy(emb.at[pl.ds(pl.multiple_of(first, 16), 2 * piece)], own, sem)
    copy.start()
    degree = degrees[0][...]
    for other in degrees[1:]:
        degree = degree + other[...]
    scale = 1.0 / jnp.maximum(degree, 1.0)
    for t in range(half_tiles):
        row = jnp.broadcast_to(scale[t * 8 : t * 8 + 1, :], (TILE, TILE))
        inverse[t * TILE : (t + 1) * TILE, :] = row.T
    copy.wait()
    for h, (group, out) in enumerate(((low, out_low), (high, out_high))):
        summed = group[0][...]
        for other in group[1:]:
            summed = summed + other[...].astype(F32)
        at = pl.multiple_of(me * 2 * piece + h * piece, 8)
        factor = inverse[pl.ds(at, piece), :]
        width = summed.shape[1] // TILE
        mean = (summed * jnp.concatenate([factor] * width, axis=1)).astype(BF16)
        projected = jnp.dot(mean, weight[...], preferred_element_type=F32)
        kept = own[h * piece : (h + 1) * piece, :].astype(F32)
        out[...] = (kept + silu(projected)).astype(BF16)


def refresh(low, high, degrees, weight, user_emb, n_edge):
    piece, channels = low[0].shape
    half_tiles = user_emb.shape[0] // TILE // n_edge
    shape = jax.ShapeDtypeStruct((piece, channels), BF16)
    count = len(low) + len(high) + len(degrees) + 1
    return pl.pallas_call(
        functools.partial(refresh_body, (len(low), len(high)), len(degrees), half_tiles),
        out_shape=[shape, shape],
        in_specs=[VMEM] * count + [ANY],
        out_specs=[VMEM] * 2,
        scratch_shapes=[
            pltpu.VMEM((2 * piece, channels), BF16),
            pltpu.VMEM((half_tiles * TILE, TILE), F32),
            pltpu.SemaphoreType.DMA(()),
        ],
        name="refresh",
    )(*low, *high, *degrees, weight, user_emb)


def chunk_order(place, n_user):
    if n_user == 4:
        upper = place >= 2
        return [place, jnp.bitwise_xor(place, 1), jnp.where(upper, 1, 2), jnp.where(upper, 0, 3)]
    return [jnp.bitwise_xor(place, k) for k in range(n_user)]


def hop_two_kernel(n_item, n_user, n_edge, item_tiles, *refs):
    lists = [refs[3 * e : 3 * e + 3] for e in range(n_edge)]
    refs = refs[3 * n_edge :]
    links, refs = refs[:n_edge], refs[n_edge:]
    total_pieces = n_edge * n_item * 2
    pieces, refs = refs[:total_pieces], refs[total_pieces:]
    outs, refs = refs[:n_user], refs[n_user:]
    counts, total, held, rows, slot_of, source_of, target_of, sem = refs
    slots = links[0].shape[0]
    me, core, place = lax.axis_index("item"), lax.axis_index("edge"), lax.axis_index("user")
    share = item_tiles // (n_user * n_edge)
    piece = pieces[0].shape[0]
    copies = load_links(links, held, sem)
    for d in range(n_edge):
        for k in range(n_item):
            for h in range(2):
                number = (d * n_item + k) * 2 + h
                owner = jnp.bitwise_xor(core, d) * n_item + jnp.bitwise_xor(me, k)
                first = pl.multiple_of((owner * 2 + h) * piece, 16)
                copies.append(
                    pltpu.make_async_copy(
                        pieces[number], rows.at[pl.ds(first, piece)], sem.at[n_edge + number]
                    )
                )
                copies[-1].start()

    def pick(item, user):
        whose = item // share
        target = (whose // n_edge) * share + item % share
        return user, target, whose % n_edge == core

    groups = choose_slots(lists, slots, pick, slot_of, source_of, target_of)
    for t in range(item_tiles):
        counts[t] = 0
    for items, _, count in lists:

        def tally(b, carry, items=items):
            counts[items[b]] += 1
            return carry

        lax.fori_loop(0, count[0], tally, 0)
    total[...] = jnp.zeros_like(total)
    for copy in copies:
        copy.wait()
    inside = lax.broadcasted_iota(jnp.int32, (TILE, TILE), 0)

    def step(g, carry):
        for i in range(GROUP):
            at = g * GROUP + i
            link = held[pl.ds(slot_of[at], 1), :]
            onehot = jnp.where(inside == link, 1.0, 0.0).astype(BF16)
            source = pl.multiple_of(source_of[at] * TILE, TILE)
            target = pl.multiple_of(target_of[at] * TILE, TILE)
            part = lax.dot_general(
                onehot,
                rows[pl.ds(source, TILE), :],
                (((0,), (0,)), ((), ())),
                preferred_element_type=F32,
            )
            total[pl.ds(target, TILE), :] += part
        return carry

    lax.fori_loop(0, groups, step, 0)
    span = share * TILE
    for out, chunk in zip(outs, chunk_order(place, n_user)):
        first = pl.multiple_of(chunk * span, span)
        out[...] = total[pl.ds(first, span), :].astype(out.dtype)


def hop_two(lists, links, pieces, n_item, n_user, n_edge, item_tiles):
    slots, channels = links[0].shape[0], pieces[0].shape[1]
    users = len(pieces) * pieces[0].shape[0]
    span = item_tiles // (n_user * n_edge) * TILE
    shapes = [
        jax.ShapeDtypeStruct((span, channels), F32 if k == 0 else BF16) for k in range(n_user)
    ]
    shapes.append(jax.ShapeDtypeStruct((item_tiles,), jnp.int32))
    room = n_edge * slots + GROUP
    return pl.pallas_call(
        functools.partial(hop_two_kernel, n_item, n_user, n_edge, item_tiles),
        out_shape=shapes,
        in_specs=[SMEM] * (3 * n_edge) + [ANY] * (n_edge + len(pieces)),
        out_specs=[VMEM] * n_user + [SMEM],
        scratch_shapes=[
            pltpu.VMEM((n_user * span, channels), F32),
            pltpu.VMEM((n_edge * slots + 8, TILE), jnp.int32),
            pltpu.VMEM((users, channels), BF16),
            pltpu.SMEM((room,), jnp.int32),
            pltpu.SMEM((room,), jnp.int32),
            pltpu.SMEM((room,), jnp.int32),
            pltpu.SemaphoreType.DMA((n_edge + len(pieces),)),
        ],
        name="hop_two",
    )(*[part for entry in lists for part in entry], *links, *pieces)


def finish_kernel(n_sums, n_counts, n_edge, *refs):
    sums, refs = refs[:n_sums], refs[n_sums:]
    counts, refs = refs[:n_counts], refs[n_counts:]
    up, down, emb, out, own, sem = refs
    place = lax.axis_index("user") * n_edge + lax.axis_index("edge")
    span = out.shape[0]
    copy = pltpu.make_async_copy(
        emb.at[pl.ds(pl.multiple_of(place * span, span), span)], own, sem
    )
    copy.start()
    copy.wait()
    for t in range(span // TILE):
        rows = slice(t * TILE, (t + 1) * TILE)
        number = counts[0][place * (span // TILE) + t]
        for other in counts[1:]:
            number = number + other[place * (span // TILE) + t]
        degree = jnp.full((TILE, 1), jnp.maximum(number, 1), jnp.int32).astype(F32)
        summed = sums[0][rows, :]
        for other in sums[1:]:
            summed = summed + other[rows, :].astype(F32)
        merged = own[rows, :].astype(F32) + summed / degree
        hidden = silu(jnp.dot(merged.astype(BF16), up[...], preferred_element_type=F32))
        added = jnp.dot(hidden.astype(BF16), down[...], preferred_element_type=F32)
        out[rows, :] = (merged + added).astype(BF16)


def finish(sums, counts, up, down, item_emb, n_edge):
    span, channels = sums[0].shape
    return pl.pallas_call(
        functools.partial(finish_kernel, len(sums), len(counts), n_edge),
        out_shape=jax.ShapeDtypeStruct((span, channels), BF16),
        in_specs=[VMEM] * len(sums) + [SMEM] * len(counts) + [VMEM, VMEM, ANY],
        out_specs=VMEM,
        scratch_shapes=[pltpu.VMEM((span, channels), BF16), pltpu.SemaphoreType.DMA(())],
        name="finish",
    )(*sums, *counts, up, down, item_emb)


def swap(value, axis, size, k):
    return lax.ppermute(value, axis, [(i, i ^ k) for i in range(size)])


def add(a, b):
    return (a.astype(F32) + b.astype(F32)).astype(BF16)


def doubled(value, axis, size):
    k, other = 1, None
    while k < size:
        if other is not None:
            value = value + other
        other = swap(value, axis, size, k)
        k *= 2
    return [value] if other is None else [value, other]


def gather_sums(pieces, size):
    if size == 4:
        (own_low, own_high), (x_low, x_high), (y_low, y_high), (d_low, d_high) = pieces
        move = lambda value, k: swap(value, "item", size, k)
        a1, b1 = move(d_low, 1), move(d_high, 2)
        a2, b2 = move(x_low, 1), move(y_high, 2)
        r1, r2 = move(add(y_low, a1), 2), move(add(x_high, b1), 1)
        return [own_low, a2, r1], [own_high, b2, r2]
    low, high = [pieces[0][0]], [pieces[0][1]]
    for k in range(1, size):
        low.append(swap(pieces[k][0], "item", size, k))
        high.append(swap(pieces[k][1], "item", size, k))
    return low, high


def spread(low, high, size):
    move = lambda value, k: swap(value, "item", size, k)
    if size == 4:
        x_low, y_high = move(low, 1), move(high, 2)
        x_high, y_low = move(high, 1), move(low, 2)
        d_low, d_high = move(x_low, 2), move(y_high, 1)
        return [low, high, x_low, x_high, y_low, y_high, d_low, d_high]
    out = [low, high]
    for k in range(1, size):
        out += [move(low, k), move(high, k)]
    return out


def collect_items(chunks, size):
    move = lambda value, pairs: lax.ppermute(value, "user", pairs)
    if size == 4:
        own, pair, cross, far = chunks
        first = move(far, [(0, 1), (3, 2)])
        near = move(cross, [(1, 2), (2, 1)])
        side = swap(pair, "user", size, 1)
        long = move(cross, [(0, 2), (3, 1)])
        last = move(add(far, first), [(1, 3), (2, 0)])
        return [own, near, side, long, last]
    return [chunks[0]] + [swap(chunks[k], "user", size, k) for k in range(1, size)]


def body(
    sizes,
    item_emb,
    user_emb,
    block_item,
    block_user,
    block_rows,
    block_count,
    user_weight,
    up_weight,
    down_weight,
):
    n_item, n_user, n_edge = sizes
    item_tiles = item_emb.shape[0] // TILE
    user_tiles = user_emb.shape[0] // TILE
    mine = (block_item.reshape(-1), block_user.reshape(-1), block_count.reshape(-1))
    mine_links = block_rows.reshape(-1, TILE)
    lists, links = [mine], [mine_links]
    for k in range(1, n_edge):
        lists.append(tuple(swap(part, "edge", n_edge, k) for part in mine))
        links.append(swap(mine_links, "edge", n_edge, k))
    *parts, hits = hop_one(lists, links, item_emb, n_item, n_edge, user_tiles)
    parts = [tuple(parts[2 * k : 2 * k + 2]) for k in range(n_item)]
    low, high = gather_sums(parts, n_item)
    degrees = doubled(hits, "item", n_item)
    new_low, new_high = refresh(low, high, degrees, user_weight, user_emb, n_edge)
    pieces = spread(new_low, new_high, n_item)
    everything = list(pieces)
    for k in range(1, n_edge):
        everything += [swap(piece, "edge", n_edge, k) for piece in pieces]
    *chunks, tally = hop_two(lists, links, everything, n_item, n_user, n_edge, item_tiles)
    sums = collect_items(chunks, n_user)
    counts = doubled(tally, "user", n_user)
    return finish(sums, counts, up_weight, down_weight, item_emb, n_edge)


def solution(mesh):
    sizes = tuple(mesh.shape[name] for name in ("item", "user", "edge"))
    return jax.shard_map(
        functools.partial(body, sizes),
        mesh=mesh,
        in_specs=(
            P("item", None),
            P("user", None),
            P("item", "user", "edge", None),
            P("item", "user", "edge", None),
            P("item", "user", "edge", None, None),
            P("item", "user", "edge"),
            P(),
            P(),
            P(),
        ),
        out_specs=P(("item", "user", "edge"), None),
        check_vma=False,
    )
```
